32 devices in a mesh: seq: 8 (over y, x, core), head: 4 (over z).
Axes of the slice: x: 2, y: 2, z: 4, core: 2. Of those that a mesh axis runs over, the one named last changes fastest.
Arguments:
- hidden_in: float32 [4096, 768], P('seq'), may hold values from -6 to 6
- grad_out: float32 [4096, 768], P('seq'), may hold values from -6 to 6
- doc_lengths: int32 [3], replicated, may hold values from 1 to 2048, as said below
- norm_gain: float32 [2, 768], replicated, may hold values from 0.5 to 1.5
- proj_z: float32 [2, 768, 1536], P(None, 'seq', 'head'), may hold values from -0.21875 to 0.21875
- proj_x: float32 [2, 768, 1536], P(None, 'seq', 'head'), may hold values from -0.21875 to 0.21875
- proj_bc: float32 [2, 768, 256], P(None, 'seq', 'head'), may hold values from -0.21875 to 0.21875
- proj_dt: float32 [2, 768, 24], P(None, 'seq', 'head'), may hold values from -0.21875 to 0.21875
- conv_x_kernel: float32 [2, 4, 1536], P(None, None, 'head'), may hold values from -3 to 3
- conv_x_bias: float32 [2, 1536], P(None, 'head'), may hold values from -0.5 to 0.5
- conv_bc_kernel: float32 [2, 4, 256], P(None, None, 'head'), may hold values from -3 to 3
- conv_bc_bias: float32 [2, 256], P(None, 'head'), may hold values from -0.5 to 0.5
- dt_bias: float32 [2, 24], P(None, 'head'), may hold values from -6 to -3
- a_log: float32 [2, 24], P(None, 'head'), may hold values from -3 to 2
- skip_gain: float32 [2, 24], P(None, 'head'), may hold values from 0.5 to 1.5
- gate_gain: float32 [2, 1536], P(None, 'head'), may hold values from 0.5 to 1.5
- proj_out: float32 [2, 768, 1536], P(None, 'seq', 'head'), may hold values from -0.15625 to 0.15625
Outputs:
- hidden_out: float32 [4096, 768], P('seq')
- grad_hidden: float32 [4096, 768], P('seq')
- grad_norm_gain: float32 [2, 768], replicated
- grad_proj_z: float32 [2, 768, 1536], P(None, 'seq', 'head')
- grad_proj_x: float32 [2, 768, 1536], P(None, 'seq', 'head')
- grad_proj_bc: float32 [2, 768, 256], P(None, 'seq', 'head')
- grad_proj_dt: float32 [2, 768, 24], P(None, 'seq', 'head')
- grad_conv_x_kernel: float32 [2, 4, 1536], P(None, None, 'head')
- grad_conv_x_bias: float32 [2, 1536], P(None, 'head')
- grad_conv_bc_kernel: float32 [2, 4, 256], P(None, None, 'head')
- grad_conv_bc_bias: float32 [2, 256], P(None, 'head')
- grad_dt_bias: float32 [2, 24], P(None, 'head')
- grad_a_log: float32 [2, 24], P(None, 'head')
- grad_skip_gain: float32 [2, 24], P(None, 'head')
- grad_gate_gain: float32 [2, 1536], P(None, 'head')
- grad_proj_out: float32 [2, 768, 1536], P(None, 'seq', 'head')
The draws below stay inside these ranges and needn't reach their ends.
Inputs may be any that keep to these rules, and one draw needn't show every extreme that they name: `doc_lengths`: the 3 lengths sum to 4096, and the longest is exactly 2048.
All inputs are finite; a program needn't handle non-finite values.
Results may differ from the reference program's by a relative error of at most 0.0003.
Values sent between devices are 32-bit elements; how exact they have to be, the bound alone decides.
A program may use at most 192 MiB of HBM per device.

```python
import jax
import jax.numpy as jnp
from jax import lax

D = 768
HEADS = 24
HEADDIM = 64
STATE = 128
KERNEL = 4
LAYERS = 2
BLOCK = 256
INNER = 1536
TOKENS = 4096
NSEQ = 3
MOST = 2048


def split_amount(key, amount_all, count_pieces):
    weights = jax.random.randint(key, (count_pieces,), 900, 1001).astype(jnp.int32)
    running = jnp.cumsum(weights).astype(jnp.int32)
    bounds = amount_all * running // running[-1]
    before = jnp.concatenate([jnp.zeros((1,), jnp.int32), bounds[:-1]])
    return (bounds - before).astype(jnp.int32)


def draw_doc_lengths(key, part):
    key_offset = jax.random.fold_in(key, 11)
    key_left = jax.random.fold_in(key, 12)
    key_right = jax.random.fold_in(key, 13)
    offset_draw = jax.random.randint(key_offset, (), -(MOST // 8), MOST // 8 + 1).astype(jnp.int32)
    left_amount = TOKENS // 2 - MOST // 2 + offset_draw
    right_amount = TOKENS - MOST - left_amount
    left_count = (NSEQ - 1) // 2
    right_count = NSEQ - 1 - left_count
    longest = jnp.full((1,), MOST, jnp.int32)
    return jnp.concatenate([split_amount(key_left, left_amount, left_count), longest, split_amount(key_right, right_amount, right_count)]).astype(jnp.int32)


def block_levels(rng, shape, shards, low, top_value):
    level, own = 1.0, jax.random.fold_in(rng, 6)
    for dim, shards_of in shards:
        heights = jnp.exp(jax.random.uniform(jax.random.fold_in(own, dim), (shards_of,), jnp.float32, low / len(shards), top_value / len(shards)))
        level = level * jnp.repeat(heights, shape[dim] // shards_of).reshape([-1 if axis == dim else 1 for axis in range(len(shape))])
    return level


def scatter_about(rng, extent, scale, bound, shards=(), kind=jnp.bfloat16):
    drawn = scale * jax.random.normal(rng, extent, jnp.float32)
    if shards:
        drawn = drawn * block_levels(rng, extent, shards, -0.22, 0.18)
    return jnp.clip(drawn, -bound, bound).astype(kind)


def setup_inputs(seed: int = 0) -> dict:
    key_list = jax.random.split(jax.random.key(seed), 18)
    hidden_in = scatter_about(key_list[0], (TOKENS, D), 1.0, 6.0, ((0, 8),), jnp.float32)
    grad_out = scatter_about(key_list[1], (TOKENS, D), 1.0, 6.0, ((0, 8),), jnp.float32)
    doc_lengths = draw_doc_lengths(jax.random.fold_in(key_list[17], 71), 0)
    norm_gain = jnp.clip(1.0 + 0.1 * jax.random.normal(key_list[3], (LAYERS, D), jnp.float32), 0.5, 1.5)
    proj_z = scatter_about(key_list[4], (LAYERS, D, INNER), D ** -0.5, 0.21875, ((1, 8), (2, 4)), jnp.float32)
    proj_x = scatter_about(key_list[5], (LAYERS, D, INNER), D ** -0.5, 0.21875, ((1, 8), (2, 4)), jnp.float32)
    proj_bc = scatter_about(key_list[6], (LAYERS, D, 2 * STATE), D ** -0.5, 0.21875, ((1, 8), (2, 4)), jnp.float32)
    proj_dt = scatter_about(key_list[7], (LAYERS, D, HEADS), D ** -0.5, 0.21875, ((1, 8), (2, 4)), jnp.float32)
    conv_x_kernel = scatter_about(key_list[8], (LAYERS, KERNEL, INNER), KERNEL ** -0.5, 3.0, ((2, 4),), jnp.float32)
    conv_x_bias = jnp.clip(jax.random.uniform(key_list[9], (LAYERS, INNER), jnp.float32, -0.5, 0.5) * block_levels(key_list[9], (LAYERS, INNER), ((1, 4),), -0.4, 0.0), -0.5, 0.5)
    conv_bc_kernel = scatter_about(key_list[10], (LAYERS, KERNEL, 2 * STATE), KERNEL ** -0.5, 3.0, ((2, 4),), jnp.float32)
    conv_bc_bias = jnp.clip(jax.random.uniform(key_list[11], (LAYERS, 2 * STATE), jnp.float32, -0.5, 0.5) * block_levels(key_list[11], (LAYERS, 2 * STATE), ((1, 4),), -0.4, 0.0), -0.5, 0.5)
    dt_bias = jnp.clip(-6.0 + 3.0 * jax.random.uniform(key_list[12], (LAYERS, HEADS), jnp.float32) ** block_levels(key_list[12], (LAYERS, HEADS), ((1, 4),), -0.2, 0.2), -6.0, -3.0)
    a_log = jnp.clip(-3.0 + 5.0 * jax.random.uniform(key_list[13], (LAYERS, HEADS), jnp.float32) ** block_levels(key_list[13], (LAYERS, HEADS), ((1, 4),), -0.2, 0.2), -3.0, 2.0)
    skip_gain = jnp.clip(0.5 + 1.0 * jax.random.uniform(key_list[14], (LAYERS, HEADS), jnp.float32) ** block_levels(key_list[14], (LAYERS, HEADS), ((1, 4),), -0.2, 0.2), 0.5, 1.5)
    gate_gain = jnp.clip(1.0 + 0.1 * jax.random.normal(key_list[15], (LAYERS, INNER), jnp.float32), 0.5, 1.5)
    proj_out = scatter_about(key_list[16], (LAYERS, D, INNER), INNER ** -0.5, 0.15625, ((1, 8), (2, 4)), jnp.float32)
    return dict(hidden_in=hidden_in, grad_out=grad_out, doc_lengths=doc_lengths, norm_gain=norm_gain, proj_z=proj_z, proj_x=proj_x, proj_bc=proj_bc, proj_dt=proj_dt, conv_x_kernel=conv_x_kernel, conv_x_bias=conv_x_bias, conv_bc_kernel=conv_bc_kernel, conv_bc_bias=conv_bc_bias, dt_bias=dt_bias, a_log=a_log, skip_gain=skip_gain, gate_gain=gate_gain, proj_out=proj_out)


EPS = 1e-05
NEG_FILL = -1e+30

def matmul_high(left, right):
    return jnp.dot(left, right, precision=lax.Precision.HIGHEST, preferred_element_type=jnp.float32)

def swish_act(values):
    return values * jax.nn.sigmoid(values)

def rms_scale(values):
    return lax.rsqrt(lax.optimization_barrier(jnp.mean(values * values, axis=-1, keepdims=True)) + EPS)

def segment_ids(doc_lengths, positions):
    lengths = doc_lengths.astype(jnp.int32)
    ends = jnp.cumsum(lengths).astype(jnp.int32)
    starts = ends - lengths
    return lax.optimization_barrier(jnp.sum((positions[:, None] >= starts[None, :]).astype(jnp.int32), axis=1)).astype(jnp.int32) - 1

def depthwise_conv(extended, seg_ext, seg_now, kernel, bias):
    count = seg_now.shape[0]
    total = jnp.zeros((count, extended.shape[1]), jnp.float32) + bias[None, :]
    for offset in range(KERNEL):
        keep = (seg_ext[offset:offset + count] == seg_now).astype(jnp.float32)
        total = total + kernel[offset][None, :] * extended[offset:offset + count] * keep[:, None]
    return swish_act(total)

def decay_rates(dt_raw, dt_bias, a_log):
    step_size = jax.nn.softplus(dt_raw + dt_bias)
    return (step_size, -step_size * jnp.exp(a_log))

def block_step(state, seg_prev, values, step_size, log_decay, b_matrix, c_matrix, seg_now):
    count, width = values.shape
    heads = step_size.shape[1]
    head_dim = width // heads
    cum_decay = jnp.cumsum(log_decay, axis=0)
    order = jnp.arange(count)
    allowed = (order[:, None] >= order[None, :]) & (seg_now[:, None] == seg_now[None, :])
    spans = cum_decay.T[:, :, None] - cum_decay.T[:, None, :]
    decays = jnp.exp(jnp.where(allowed[None], spans, NEG_FILL))
    intersection = matmul_high(c_matrix, b_matrix.T)
    scores = decays * intersection[None] * step_size.T[:, None, :]
    per_head = values.reshape(count, heads, head_dim)
    output = jnp.einsum('hts,shp->thp', scores, per_head, precision=lax.Precision.HIGHEST).reshape(count, width)
    enter = jnp.exp(cum_decay) * (seg_now == seg_prev).astype(jnp.float32)[:, None]
    output = output + jnp.repeat(enter, head_dim, axis=1) * matmul_high(c_matrix, state.T)
    keep_end = (seg_now == seg_now[-1]).astype(jnp.float32)
    weight_end = jnp.exp(cum_decay[-1][None, :] - cum_decay) * step_size * keep_end[:, None]
    weighted = values * jnp.repeat(weight_end, head_dim, axis=1)
    carry = jnp.exp(cum_decay[-1]) * (seg_now[-1] == seg_prev).astype(jnp.float32)
    state = state * jnp.repeat(carry, head_dim)[:, None] + jnp.einsum('tc,tn->cn', weighted, b_matrix, precision=lax.Precision.HIGHEST)
    return (state, seg_now[-1], output)

def ssd_scan(values, step_size, log_decay, b_matrix, c_matrix, seg_now):
    count = values.shape[0]
    blocks = count // BLOCK

    def one_block(carry, pieces):
        state, seg_prev = carry
        state, seg_last, output = block_step(state, seg_prev, *pieces)
        return ((state, seg_last), output)
    pieces = tuple((array_in.reshape((blocks, BLOCK) + array_in.shape[1:]) for array_in in (values, step_size, log_decay, b_matrix, c_matrix, seg_now)))
    start = (jnp.zeros((values.shape[1], STATE), jnp.float32), jnp.zeros((), jnp.int32))
    _, outputs = lax.scan(jax.checkpoint(one_block), start, pieces)
    return outputs.reshape(count, values.shape[1])

def pad_front(raw):
    return jnp.concatenate([jnp.zeros((KERNEL - 1, raw.shape[1]), jnp.float32), raw], axis=0)

def layer_forward(hidden, seg_ext, seg_now, params):
    norm_gain, proj_z, proj_x, proj_bc, proj_dt, conv_x_kernel, conv_x_bias, conv_bc_kernel, conv_bc_bias, dt_bias, a_log, skip_gain, gate_gain, proj_out = params
    normed = hidden * rms_scale(hidden) * norm_gain[None, :]
    gate_in = matmul_high(normed, proj_z)
    x_raw = matmul_high(normed, proj_x)
    bc_raw = matmul_high(normed, proj_bc)
    dt_raw = matmul_high(normed, proj_dt)
    values = depthwise_conv(pad_front(x_raw), seg_ext, seg_now, conv_x_kernel, conv_x_bias)
    bc_act = depthwise_conv(pad_front(bc_raw), seg_ext, seg_now, conv_bc_kernel, conv_bc_bias)
    step_size, log_decay = decay_rates(dt_raw, dt_bias, a_log)
    mixed = ssd_scan(values, step_size, log_decay, bc_act[:, :STATE], bc_act[:, STATE:], seg_now)
    mixed = mixed + jnp.repeat(skip_gain, HEADDIM)[None, :] * values
    gated = mixed * swish_act(gate_in)
    normed_out = gated * rms_scale(gated) * gate_gain[None, :]
    return hidden + matmul_high(normed_out, proj_out.T)

def reference(hidden_in, grad_out, doc_lengths, norm_gain, proj_z, proj_x, proj_bc, proj_dt, conv_x_kernel, conv_x_bias, conv_bc_kernel, conv_bc_bias, dt_bias, a_log, skip_gain, gate_gain, proj_out):
    positions = jnp.arange(-(KERNEL - 1), TOKENS, dtype=jnp.int32)
    seg_ext = segment_ids(doc_lengths, positions)
    seg_now = seg_ext[KERNEL - 1:]
    weights = (norm_gain, proj_z, proj_x, proj_bc, proj_dt, conv_x_kernel, conv_x_bias, conv_bc_kernel, conv_bc_bias, dt_bias, a_log, skip_gain, gate_gain, proj_out)

    def one_layer(hidden, params):
        return layer_forward(hidden, seg_ext, seg_now, params)
    layer_ckpt = jax.checkpoint(one_layer)

    def whole(hidden, params_all):
        for layer_idx in range(LAYERS):
            hidden = layer_ckpt(hidden, tuple((tensor[layer_idx] for tensor in params_all)))
        return hidden
    hidden_out, pullback = jax.vjp(whole, hidden_in, weights)
    grad_hidden, grads = pullback(grad_out)
    g_norm, g_z, g_x, g_bc, g_dt, g_cxk, g_cxb, g_cbk, g_cbb, g_dtb, g_alog, g_skip, g_gate, g_out = grads
    return (hidden_out, grad_hidden, g_norm, g_z, g_x, g_bc, g_dt, g_cxk, g_cxb, g_cbk, g_cbb, g_dtb, g_alog, g_skip, g_gate, g_out)
```

```python
from functools import partial

import jax
import jax.numpy as jnp
from jax import lax
from jax.sharding import PartitionSpec as P

STATE = 128
KERNEL = 4
BLOCK = 256


EPS = 1e-05
NEG_FILL = -1e30
EXACT = lax.Precision.HIGHEST
FAST = lax.Precision.HIGH


def passed_along(array, axis, by):
    count = lax.axis_size(axis)
    pairs = [(i, i + by) for i in range(count) if 0 <= i + by < count]
    return lax.ppermute(array, axis, pairs)


def product(spec, left, right, precision=FAST):
    return jnp.einsum(spec, left, right, precision=precision, preferred_element_type=jnp.float32)


def swish_act(values):
    return values * jax.nn.sigmoid(values)


def rms_scale(values):
    return lax.rsqrt(jnp.mean(values * values, axis=-1, keepdims=True) + EPS)


def segment_ids(doc_lengths, positions):
    ends = jnp.cumsum(doc_lengths)
    starts = ends - doc_lengths
    return jnp.sum((positions[:, None] >= starts[None, :]).astype(jnp.int32), axis=1) - 1


def widened(per_head, width):
    heads = per_head.shape[1]
    owner = jnp.arange(width) // (width // heads)
    spread = (jnp.arange(heads)[:, None] == owner[None, :]).astype(jnp.float32)
    return product("th,hc->tc", per_head, spread, EXACT)


def scaled_heads(state, factors):
    heads = factors.shape[0]
    return (state.reshape(heads, -1, state.shape[-1]) * factors[:, None, None]).reshape(state.shape)


def entering(pieces, decays, backward):
    count, mine = (lax.axis_size("seq"), lax.axis_index("seq"))
    order = jnp.arange(count)
    first, middle = (order[:, None], order[None, :])
    if backward:
        between = (middle > mine) & (middle < first)
        outside = order > mine
    else:
        between = (middle > first) & (middle < mine)
        outside = order < mine
    weights = jnp.prod(jnp.where(between[..., None], decays[None], 1.0), axis=1)
    weights = jnp.where(outside[:, None], weights, 0.0)
    heads = decays.shape[1]
    split = pieces.reshape(count, heads, -1, pieces.shape[-1])
    return jnp.sum(split * weights[:, :, None, None], axis=0).reshape(pieces.shape[1:])


def with_rows(rows, extra):
    width = rows.shape[1]
    more = -(-extra.shape[0] // (8 * width)) * 8
    return jnp.concatenate(
        [rows, jnp.pad(extra, (0, more * width - extra.shape[0])).reshape(more, width)], axis=0
    )


def front_fn(hidden, gain, weight_zx, weight_bd, inner_loc):
    normed = hidden * rms_scale(hidden) * gain[None, :]
    main = product("td,dc->tc", normed, weight_zx)
    side = product("td,dc->tc", normed, weight_bd)
    raw = jnp.concatenate([main[:, inner_loc:], side[:, : 2 * STATE]], axis=1)
    return (main[:, :inner_loc], raw, side[:, 2 * STATE :])


def conv_local(raw, prev_tail, kernel, bias, keeps):
    extended = jnp.concatenate([prev_tail, raw], axis=0)
    count = raw.shape[0]
    total = jnp.zeros_like(raw) + bias[None, :]
    for offset in range(KERNEL):
        total = total + kernel[offset][None, :] * extended[offset : offset + count] * keeps[offset]
    return swish_act(total)


def local_fn(values, dt_raw, dt_bias, a_log, skip_gain, bc, seg_now, seg_prev):
    count, width = values.shape
    heads = dt_raw.shape[1]
    rows = min(BLOCK, count)
    blocks = count // rows
    step_size = jax.nn.softplus(dt_raw + dt_bias)
    log_decay = -step_size * jnp.exp(a_log)
    order = jnp.arange(rows)
    lower = order[:, None] >= order[None, :]
    cum = product(
        "ts,bsh->bth",
        lower.astype(jnp.float32),
        log_decay.reshape(blocks, rows, heads),
        EXACT,
    )
    cum_rows = cum.transpose(2, 0, 1)
    seg = seg_now.reshape(blocks, rows)
    before = jnp.concatenate([seg_prev[None], seg[:-1, -1]])
    allowed = lower[None] & (seg[:, :, None] == seg[:, None, :])
    spans = cum_rows[:, :, :, None] - cum_rows[:, :, None, :]
    decays = jnp.exp(jnp.where(allowed[None], spans, NEG_FILL))
    b_matrix = bc[:, :STATE].reshape(blocks, rows, STATE)
    c_matrix = bc[:, STATE:].reshape(blocks, rows, STATE)
    scores = decays * product("btn,bsn->bts", c_matrix, b_matrix)[None]
    stepped = values * widened(step_size, width)
    output = product(
        "hbts,bshp->bthp", scores, stepped.reshape(blocks, rows, heads, width // heads)
    ).reshape(count, width)
    output = output + jnp.repeat(skip_gain, width // heads)[None, :] * values
    last = cum[:, -1]
    enter = jnp.exp(cum) * (seg == before[:, None]).astype(jnp.float32)[..., None]
    keep_end = (seg == seg[:, -1:]).astype(jnp.float32)
    leave = jnp.exp(last[:, None] - cum) * keep_end[..., None]
    weighted = stepped * widened(leave.reshape(count, heads), width)
    states = product("bsc,bsn->bcn", weighted.reshape(blocks, rows, width), b_matrix)
    carries = jnp.exp(last) * (seg[:, -1] == before).astype(jnp.float32)[:, None]
    state, decay = (states[0], carries[0])
    for block in range(1, blocks):
        state = scaled_heads(state, carries[block]) + states[block]
        decay = decay * carries[block]
    return (output, enter.reshape(count, heads), states, carries, state, decay)


def mix_fn(output, enter, states, carries, state_in, bc):
    count, width = output.shape
    blocks = states.shape[0]
    entry = [state_in]
    for block in range(blocks - 1):
        entry.append(scaled_heads(entry[-1], carries[block]) + states[block])
    c_matrix = bc[:, STATE:].reshape(blocks, count // blocks, STATE)
    read = product("btn,bcn->btc", c_matrix, jnp.stack(entry)).reshape(count, width)
    return output + widened(enter, width) * read


def gate_fn(mixed, gate_in, gate_gain, proj_out_loc):
    gated = mixed * swish_act(gate_in)
    rows = product("tc,dc->td", gated * gate_gain[None, :], proj_out_loc)
    return (rows, jnp.sum(gated * gated, axis=1))


def body(
    hidden_in,
    grad_out,
    doc_lengths,
    norm_gain,
    proj_z,
    proj_x,
    proj_bc,
    proj_dt,
    conv_x_kernel,
    conv_x_bias,
    conv_bc_kernel,
    conv_bc_bias,
    dt_bias,
    a_log,
    skip_gain,
    gate_gain,
    proj_out,
):
    count, width = hidden_in.shape
    layers, rows_loc, inner_loc = proj_z.shape
    bc_loc = proj_bc.shape[2]
    heads = proj_dt.shape[2]
    inner = inner_loc * lax.axis_size("head")
    bc_all = 2 * STATE
    margin = KERNEL - 1
    positions = lax.axis_index("seq") * count + jnp.arange(-margin, count, dtype=jnp.int32)
    seg_ext = segment_ids(doc_lengths, positions)
    seg_now = seg_ext[margin:]
    seg_prev = seg_ext[margin - 1]
    keeps = [
        (seg_ext[offset : offset + count] == seg_now).astype(jnp.float32)[:, None]
        for offset in range(KERNEL)
    ]

    def over_seq(part):
        return lax.all_gather(part, "seq", axis=0, tiled=True)

    columns = lax.all_gather(
        jnp.concatenate([proj_bc, conv_bc_kernel, conv_bc_bias[:, None]], axis=1),
        "head",
        axis=2,
        tiled=True,
    )
    first = over_seq(
        jnp.concatenate(
            [proj_z[0], proj_x[0]]
            + [
                part
                for layer in range(layers)
                for part in (columns[layer, :rows_loc], proj_dt[layer])
            ],
            axis=1,
        )
    )
    rest = over_seq(
        jnp.concatenate(
            [proj_out[0]]
            + [
                part
                for layer in range(1, layers)
                for part in (proj_z[layer], proj_x[layer], proj_out[layer])
            ],
            axis=1,
        )
    )
    full_zx = [first[:, : 2 * inner_loc]]
    full_out = [rest[:, :inner_loc]]
    for layer in range(1, layers):
        at = (3 * layer - 2) * inner_loc
        full_zx.append(rest[:, at : at + 2 * inner_loc])
        full_out.append(rest[:, at + 2 * inner_loc : at + 3 * inner_loc])
    side = first[:, 2 * inner_loc :]
    side_width = bc_all + heads
    full_bd = [side[:, layer * side_width : (layer + 1) * side_width] for layer in range(layers)]

    hidden = hidden_in
    saved = []
    for layer in range(layers):
        front_out, pull_front = jax.vjp(
            partial(front_fn, inner_loc=inner_loc),
            hidden,
            norm_gain[layer],
            full_zx[layer],
            full_bd[layer],
        )
        gate_in, raw, dt_raw = front_out
        prev_tail = passed_along(raw[count - margin :], "seq", 1)
        kernel = jnp.concatenate(
            [conv_x_kernel[layer], columns[layer, rows_loc : rows_loc + KERNEL]], axis=1
        )
        bias = jnp.concatenate([conv_x_bias[layer], columns[layer, rows_loc + KERNEL]])
        conv_out, pull_conv = jax.vjp(
            partial(conv_local, keeps=keeps), raw, prev_tail, kernel, bias
        )
        values, bc = (conv_out[:, :inner_loc], conv_out[:, inner_loc:])
        local_out, pull_local = jax.vjp(
            partial(local_fn, seg_now=seg_now, seg_prev=seg_prev),
            values,
            dt_raw,
            dt_bias[layer],
            a_log[layer],
            skip_gain[layer],
            bc,
        )
        output, enter, states, carries, state_dev, decay_dev = local_out
        packed = jnp.concatenate(
            [state_dev, jnp.pad(decay_dev[None], ((0, 7), (0, STATE - heads)))], axis=0
        )
        pieces = lax.all_gather(packed, "seq")
        decays = pieces[:, inner_loc, :heads]
        state_in = entering(pieces[:, :inner_loc], decays, False)
        mixed, pull_mix = jax.vjp(mix_fn, output, enter, states, carries, state_in, bc)
        (rows, squares), pull_gate = jax.vjp(
            gate_fn, mixed, gate_in, gate_gain[layer], full_out[layer]
        )
        if layer < layers - 1:
            summed = lax.psum(with_rows(rows, squares), "head")
            total_sq = summed[count:].reshape(-1)[:count]
            scale = lax.rsqrt(total_sq / inner + EPS)
            sums = summed[:count]
            hidden = hidden + scale[:, None] * sums
            grad_scale = sums
        else:
            pair = lax.psum(
                jnp.stack([squares, jnp.sum(grad_out * rows, axis=1)]), "head"
            )
            total_sq, grad_scale = (pair[0], pair[1])
            scale = lax.rsqrt(total_sq / inner + EPS)
            last_rows = scale[:, None] * rows
        saved.append(
            (
                pull_front,
                pull_conv,
                pull_local,
                pull_mix,
                pull_gate,
                scale,
                grad_scale,
                decays,
                state_in,
            )
        )

    grad_hidden = grad_out
    big, small = ([None] * layers for _ in range(2))
    own_bc = []
    for layer in reversed(range(layers)):
        (
            pull_front,
            pull_conv,
            pull_local,
            pull_mix,
            pull_gate,
            scale,
            grad_scale,
            decays,
            state_in,
        ) = saved[layer]
        if layer < layers - 1:
            grad_scale = jnp.sum(grad_hidden * grad_scale, axis=1)
        grad_squares = grad_scale * (-0.5 / inner) * scale * scale * scale
        grad_mixed, grad_gate_in, grad_ggain, grad_full_out = pull_gate(
            (scale[:, None] * grad_hidden, grad_squares)
        )
        grad_output, grad_enter, grad_states, grad_carries, grad_state_in, mix_bc = pull_mix(
            grad_mixed
        )
        grad_pieces = lax.all_gather(grad_state_in, "seq")
        if layer == layers - 1:
            grad_pieces, last_rows = lax.optimization_barrier((grad_pieces, last_rows))
            hidden_out = hidden + lax.psum(last_rows, "head")
        grad_state_end = entering(grad_pieces, decays, True)
        grad_decay = jnp.sum((grad_state_end * state_in).reshape(heads, -1), axis=1)
        grad_values, grad_dt_raw, grad_dbias, grad_alog, grad_skip, local_bc = pull_local(
            (grad_output, grad_enter, grad_states, grad_carries, grad_state_end, grad_decay)
        )
        grad_raw, grad_prev, grad_kernel, grad_cbias = pull_conv(
            jnp.concatenate([grad_values, mix_bc + local_bc], axis=1)
        )
        from_right = passed_along(grad_prev, "seq", -1)
        grad_raw = grad_raw + jnp.pad(from_right, ((count - margin, 0), (0, 0)))
        grad_part, grad_ngain, grad_zx, grad_bd = pull_front((grad_gate_in, grad_raw, grad_dt_raw))
        shared = jnp.concatenate(
            [grad_ngain, grad_kernel[:, inner_loc:].reshape(-1), grad_cbias[inner_loc:]]
        )
        if layer == layers - 1:
            grad_part, hidden_out = lax.optimization_barrier((grad_part, hidden_out))
        summed = lax.psum(with_rows(grad_part, shared), "head")
        grad_hidden = grad_hidden + summed[:count]
        shared = summed[count:].reshape(-1)[: shared.shape[0]]
        big[layer] = lax.psum_scatter(
            jnp.concatenate([grad_full_out, grad_zx, grad_bd], axis=1),
            "seq",
            scatter_dimension=0,
            tiled=True,
        )
        own_bc.append(
            lax.psum_scatter(
                big[layer][:, 3 * inner_loc : 3 * inner_loc + bc_all],
                "head",
                scatter_dimension=1,
                tiled=True,
            )
        )
        small[layer] = (
            grad_kernel[:, :inner_loc].reshape(-1),
            grad_cbias[:inner_loc],
            grad_ggain,
            grad_dbias,
            grad_alog,
            grad_skip,
            shared[:width],
            shared[width : width + KERNEL * bc_all],
            shared[width + KERNEL * bc_all :],
        )

    def laid_out(parts):
        sizes = [part.shape[0] for part in parts[0]]
        stacked = jnp.stack([jnp.concatenate(layer_parts) for layer_parts in parts])
        return (stacked, sizes)

    def taken(stacked, sizes):
        starts = [sum(sizes[:place]) for place in range(len(sizes))]
        return [stacked[:, start : start + size] for start, size in zip(starts, sizes)]

    stacked, sizes = laid_out(small)
    cxk, cxb, ggain, dbias, alog, skip, ngain, cbk, cbb = taken(lax.psum(stacked, "seq"), sizes)
    offset = lax.axis_index("head") * bc_loc
    cbk = lax.dynamic_slice_in_dim(cbk.reshape(layers, KERNEL, bc_all), offset, bc_loc, axis=2)
    cbb = lax.dynamic_slice_in_dim(cbb, offset, bc_loc, axis=1)
    return (
        hidden_out,
        grad_hidden,
        ngain,
        jnp.stack([part[:, inner_loc : 2 * inner_loc] for part in big]),
        jnp.stack([part[:, 2 * inner_loc : 3 * inner_loc] for part in big]),
        jnp.stack(own_bc[::-1]),
        jnp.stack([part[:, 3 * inner_loc + bc_all :] for part in big]),
        cxk.reshape(layers, KERNEL, inner_loc),
        cxb,
        cbk,
        cbb,
        dbias,
        alog,
        skip,
        ggain,
        jnp.stack([part[:, :inner_loc] for part in big]),
    )


def solution(mesh):
    in_specs = (
        P("seq", None),
        P("seq", None),
        P(),
        P(),
        P(None, "seq", "head"),
        P(None, "seq", "head"),
        P(None, "seq", "head"),
        P(None, "seq", "head"),
        P(None, None, "head"),
        P(None, "head"),
        P(None, None, "head"),
        P(None, "head"),
        P(None, "head"),
        P(None, "head"),
        P(None, "head"),
        P(None, "head"),
        P(None, "seq", "head"),
    )
    out_specs = (
        P("seq", None),
        P("seq", None),
        P(),
        P(None, "seq", "head"),
        P(None, "seq", "head"),
        P(None, "seq", "head"),
        P(None, "seq", "head"),
        P(None, None, "head"),
        P(None, "head"),
        P(None, None, "head"),
        P(None, "head"),
        P(None, "head"),
        P(None, "head"),
        P(None, "head"),
        P(None, "head"),
        P(None, "seq", "head"),
    )
    return jax.shard_map(body, mesh=mesh, in_specs=in_specs, out_specs=out_specs, check_vma=False)
```
